32 devices in a mesh: ctx: 8 (over y, x, core), chan: 4 (over z).
Axes of the slice: x: 2, y: 2, z: 4, core: 2. Of those that a mesh axis runs over, the one named last changes fastest.
Arguments:
- value_branch: bfloat16 [192, 65536], P(None, ('ctx', 'chan')), may hold values from -6 to 6
- key_branch: bfloat16 [192, 65536], P(None, ('ctx', 'chan')), may hold values from -6 to 6
- gate_branch: bfloat16 [192, 65536], P(None, ('ctx', 'chan')), may hold values from -6 to 6
- skip_gain: float32 [192], replicated, may hold values from -4 to 4
- spectra: float32 [2, 192, 8, 8192], P(None, 'chan', 'ctx'), may hold values from -6 to 6
Outputs:
- gated_output: bfloat16 [192, 65536], P(None, ('ctx', 'chan'))
The draws below stay inside these ranges and needn't reach their ends.
All inputs are finite; a program needn't handle non-finite values.
Results may differ from the reference program's by a relative error of at most 0.0054.
Values may be sent and summed in bfloat16 or wider, within the bound.
A program may use at most 64 MiB of HBM per device.

```python
import jax
import jax.numpy as jnp
import numpy as np
from jax import lax

CHANNELS = 192
SEQ_DEV = 8192
LENGTH = 65536
N_CTX = 8


def steps_of(rng, shape, cuts, least, high):
    level, own = 1.0, jax.random.fold_in(rng, 6)
    for dim, blocks in cuts:
        steps = jnp.exp(jax.random.uniform(jax.random.fold_in(own, dim), (blocks,), jnp.float32, least / len(cuts), high / len(cuts)))
        level = level * jnp.repeat(steps, shape[dim] // blocks).reshape([-1 if axis == dim else 1 for axis in range(len(shape))])
    return level


def scatter_about(key, dims, width, most, cuts=(), held_as=jnp.bfloat16):
    entries = width * jax.random.normal(key, dims, jnp.float32)
    if cuts:
        entries = entries * steps_of(key, dims, cuts, -0.22, 0.18)
    return jnp.clip(entries, -most, most).astype(held_as)


def setup_inputs(seed: int = 0) -> dict:
    keys = jax.random.split(jax.random.key(seed), 6)
    value_branch = scatter_about(keys[0], (CHANNELS, LENGTH), 1.0, 6.0, ((1, 32),))
    key_branch = scatter_about(keys[1], (CHANNELS, LENGTH), 1.0, 6.0, ((1, 32),))
    gate_branch = scatter_about(keys[2], (CHANNELS, LENGTH), 1.0, 6.0, ((1, 32),))
    skip_gain = scatter_about(keys[3], (CHANNELS,), 1.0, 4.0, (), jnp.float32)
    spectra = scatter_about(keys[4], (2, CHANNELS, N_CTX, SEQ_DEV), 1.0, 6.0, ((1, 4), (2, 8)), jnp.float32)
    return dict(value_branch=value_branch, key_branch=key_branch, gate_branch=gate_branch, skip_gain=skip_gain, spectra=spectra)


def reversed_bits(numbers, bit_count):
    result = numbers * 0
    for bit_number in range(bit_count):
        result = result + ((numbers >> bit_number) & 1) * (1 << (bit_count - 1 - bit_number))
    return result


def reference(value_branch, key_branch, gate_branch, skip_gain, spectra):
    carried = (key_branch.astype(jnp.float32) * value_branch.astype(jnp.float32)).astype(jnp.bfloat16)
    bit_count = N_CTX.bit_length() - 1
    reversed_order = reversed_bits(np.arange(N_CTX), bit_count)

    def convolve(packed):
        signal, filter_real, filter_imag = packed
        natural_real = jnp.swapaxes(filter_real[reversed_order, :], 0, 1).reshape(-1)
        natural_imag = jnp.swapaxes(filter_imag[reversed_order, :], 0, 1).reshape(-1)
        transformed = jnp.fft.fft(signal.astype(jnp.float32))
        shaped = transformed * (natural_real + 1j * natural_imag)
        return jnp.real(jnp.fft.ifft(shaped)).astype(jnp.float32)

    convolved = lax.map(convolve, (carried, spectra[0], spectra[1])).astype(jnp.bfloat16)
    result = gate_branch.astype(jnp.float32) * (convolved.astype(jnp.float32) + skip_gain[:, None] * carried.astype(jnp.float32))
    return result.astype(jnp.bfloat16)
```

```python
import functools
import math

import jax
import jax.numpy as jnp
import numpy as np
from jax import lax
from jax.experimental import pallas as pl
from jax.experimental.pallas import tpu as pltpu
from jax.sharding import PartitionSpec as P

two_pi = 2.0 * math.pi
first_factor = 128
highest = lax.Precision.HIGHEST


def reversed_bits(numbers, bit_count):
    result = numbers * 0
    for bit_number in range(bit_count):
        result = result + (numbers >> bit_number & 1) * (1 << bit_count - 1 - bit_number)
    return result


def phase_pair(radians):
    return (jnp.cos(radians), jnp.sin(radians))


def block_table(length_of, direction):
    counter = jnp.arange(length_of, dtype=jnp.int32)
    product = counter[:, None] * counter[None, :] % length_of
    cosine, sine = phase_pair(direction * two_pi / length_of * product.astype(jnp.float32))
    upper_rows = jnp.stack([cosine, -sine], axis=1)
    lower_rows = jnp.stack([sine, cosine], axis=1)
    return jnp.stack([upper_rows, lower_rows], axis=0)


def complex_mul(signal, factor):
    factor_real, factor_imag = factor
    return jnp.stack(
        [
            signal[0] * factor_real - signal[1] * factor_imag,
            signal[0] * factor_imag + signal[1] * factor_real,
        ]
    )


def forward_local(signal):
    channel_count, seq_length = (signal.shape[1], signal.shape[2])
    second_factor = seq_length // first_factor
    blocked = signal.reshape(2, channel_count, first_factor, second_factor)
    section_one = jnp.einsum(
        "orca,cxaq->oxrq", block_table(first_factor, -1.0), blocked, precision=highest
    )
    column = jnp.arange(first_factor, dtype=jnp.int32)[:, None]
    within = jnp.arange(second_factor, dtype=jnp.int32)[None, :]
    twiddle = phase_pair(-two_pi / seq_length * (column * within).astype(jnp.float32))
    section_two = complex_mul(section_one, twiddle)
    section_three = jnp.einsum(
        "peoq,oxrq->pxer", block_table(second_factor, -1.0), section_two, precision=highest
    )
    return section_three.reshape(2, channel_count, seq_length)


def inverse_local(signal):
    channel_count, seq_length = (signal.shape[1], signal.shape[2])
    second_factor = seq_length // first_factor
    blocked = signal.reshape(2, channel_count, second_factor, first_factor)
    section_one = jnp.einsum(
        "pqoe,oxer->pxqr", block_table(second_factor, 1.0), blocked, precision=highest
    )
    within = jnp.arange(second_factor, dtype=jnp.int32)[:, None]
    column = jnp.arange(first_factor, dtype=jnp.int32)[None, :]
    twiddle = phase_pair(two_pi / seq_length * (within * column).astype(jnp.float32))
    section_two = complex_mul(section_one, twiddle)
    section_three = jnp.einsum(
        "paor,oxqr->pxaq", block_table(first_factor, 1.0), section_two, precision=highest
    )
    return section_three.reshape(2, channel_count, seq_length)


def blockwise_body(value_branch, key_branch, gate_branch, skip_gain, spectra):
    carried = (key_branch.astype(jnp.float32) * value_branch.astype(jnp.float32)).astype(
        jnp.bfloat16
    )
    series = lax.all_to_all(carried, "chan", split_axis=0, concat_axis=1, tiled=True)
    channel_count, seq_length = series.shape
    ctx_count = lax.axis_size("ctx")
    bit_count = ctx_count.bit_length() - 1
    device = lax.axis_index("ctx")
    total_length = seq_length * ctx_count
    counter = jnp.arange(ctx_count, dtype=jnp.int32)
    target = reversed_bits(counter, bit_count)
    blocks = lax.all_to_all(
        series.reshape(channel_count, 1, seq_length), "ctx", split_axis=2, concat_axis=1, tiled=True
    )
    matrix = jnp.stack(
        phase_pair(
            -two_pi
            / ctx_count
            * (target[:, None] * counter[None, :] % ctx_count).astype(jnp.float32)
        )
    )
    rows = jnp.einsum("ojp,xps->oxjs", matrix, blocks.astype(jnp.float32), precision=highest)
    received = lax.all_to_all(rows, "ctx", split_axis=2, concat_axis=3, tiled=True)
    signal = received.reshape(2, channel_count, seq_length)
    device_rank = reversed_bits(device, bit_count)
    positions = jnp.arange(seq_length, dtype=jnp.int32)
    radians = two_pi / total_length * (positions * device_rank).astype(jnp.float32)
    signal = complex_mul(signal, phase_pair(-radians))
    spectrum = forward_local(signal)
    shaped = complex_mul(spectrum, (spectra[0, :, 0, :], spectra[1, :, 0, :]))
    returned = complex_mul(inverse_local(shaped), phase_pair(radians))
    parts = lax.all_to_all(
        returned.reshape(2, channel_count, 1, seq_length),
        "ctx",
        split_axis=3,
        concat_axis=2,
        tiled=True,
    )
    cosine, sine = phase_pair(
        two_pi / ctx_count * (counter[:, None] * target[None, :] % ctx_count).astype(jnp.float32)
    )
    matrix = jnp.stack([cosine, -sine])
    summed = jnp.einsum("opj,oxjs->xps", matrix, parts, precision=highest) / total_length
    local_conv = summed.astype(jnp.bfloat16)
    convolved = lax.all_to_all(local_conv, "ctx", split_axis=1, concat_axis=2, tiled=True).reshape(
        channel_count, seq_length
    )
    tokens_conv = lax.all_to_all(convolved, "chan", split_axis=1, concat_axis=0, tiled=True)
    result = gate_branch.astype(jnp.float32) * (
        tokens_conv.astype(jnp.float32) + skip_gain[:, None] * carried.astype(jnp.float32)
    )
    return result.astype(jnp.bfloat16)


lanes = 128
MESH = pl.DeviceIdType.MESH
VMEM = pl.BlockSpec(memory_space=pltpu.VMEM)


@functools.lru_cache(maxsize=None)
def transform_tables(rows_total, ctx_count):
    length = rows_total * lanes
    bit_count = ctx_count.bit_length() - 1
    rev = np.array([int(format(j, "b").zfill(bit_count)[::-1], 2) if bit_count else 0 for j in range(ctx_count)])
    a = np.arange(rows_total // ctx_count)
    k1 = (rev[:, None] + ctx_count * a[None, :]).reshape(-1)
    fold = lanes // (rows_total // ctx_count)
    k2 = np.arange(lanes).reshape(lanes // fold, fold).T.reshape(-1)
    n1, n2 = np.arange(rows_total), np.arange(lanes)
    f1 = np.exp(-2j * np.pi * (np.outer(k1, n1) % rows_total) / rows_total)
    f2 = np.exp(-2j * np.pi * (np.outer(n2, k2) % lanes) / lanes)
    tw = np.exp(-2j * np.pi * (np.outer(k1, n2) % length) / length)
    w1 = np.stack([f1.real, f1.imag])
    w2 = np.block([[f2.real, f2.imag], [-f2.imag, f2.real]])
    b2 = f2.conj().T
    w3 = np.block([[b2.real, b2.imag], [-b2.imag, b2.real]])
    b1 = f1.conj().T / length
    v1 = np.concatenate([b1.real, -b1.imag], axis=1)
    half = lambda t: np.asarray(t, dtype=jnp.bfloat16)
    return half(w1), half(w2), half(w3), half(v1), np.stack([tw.real, tw.imag]).astype(np.float32)


def spectra_kernel(s_ref, o_ref):
    for i in range(s_ref.shape[0]):
        turned = s_ref[i].T
        step = o_ref.shape[1]
        parts = [turned[f * step : (f + 1) * step] for f in range(turned.shape[0] // step)]
        o_ref[i] = jnp.concatenate(parts, axis=1).astype(jnp.bfloat16)


def turn_spectra(spectra):
    planes, rows, _ = spectra.shape
    block = 16
    return pl.pallas_call(
        spectra_kernel,
        grid=(planes // block,),
        in_specs=[pl.BlockSpec((block, rows, lanes), lambda i: (i, 0, 0))],
        out_specs=pl.BlockSpec((block, rows, lanes), lambda i: (i, 0, 0)),
        out_shape=jax.ShapeDtypeStruct((planes, rows, lanes), jnp.bfloat16),
    )(spectra)


def greet_all(ctx_count, chan_count, me):
    total = ctx_count * chan_count
    barrier = pltpu.get_barrier_semaphore()

    @pl.loop(1, total)
    def _(offset):
        other = lax.rem(me + offset, total)
        pl.semaphore_signal(
            barrier, inc=1, device_id=(other // chan_count, lax.rem(other, chan_count)), device_id_type=MESH
        )

    pl.semaphore_wait(barrier, total - 1)


def spread_kernel(ctx_count, chan_count, c_ref, s_ref, x_ref, r_ref, send, recv, send_s, recv_s, local):
    ctx, chan = lax.axis_index("ctx"), lax.axis_index("chan")
    me = ctx * chan_count + chan
    total = ctx_count * chan_count
    pairs, rows = x_ref.shape[0], c_ref.shape[1]
    channels, block = r_ref.shape[1], s_ref.shape[2]
    greet_all(ctx_count, chan_count, me)
    copies = []
    for offset in range(1, total):
        other = lax.rem(me + offset, total)
        other_ctx, other_chan = other // chan_count, lax.rem(other, chan_count)
        copies.append(
            pltpu.make_async_remote_copy(
                src_ref=c_ref.at[pl.ds((other_chan * ctx_count + other_ctx) * pairs, pairs)],
                dst_ref=x_ref.at[:, pl.ds(me * rows, rows)],
                send_sem=send.at[offset - 1],
                recv_sem=recv.at[offset - 1],
                device_id=(other_ctx, other_chan),
                device_id_type=MESH,
            )
        )
    for offset in range(1, ctx_count):
        other_ctx = lax.rem(ctx + offset, ctx_count)
        copies.append(
            pltpu.make_async_remote_copy(
                src_ref=s_ref.at[:, pl.ds(other_ctx * channels, channels)],
                dst_ref=r_ref.at[:, :, pl.ds(ctx * block, block)],
                send_sem=send_s.at[offset - 1],
                recv_sem=recv_s.at[offset - 1],
                device_id=(other_ctx, chan),
                device_id_type=MESH,
            )
        )
    own = [
        pltpu.make_async_copy(
            c_ref.at[pl.ds((chan * ctx_count + ctx) * pairs, pairs)], x_ref.at[:, pl.ds(me * rows, rows)], local.at[0]
        ),
        pltpu.make_async_copy(
            s_ref.at[:, pl.ds(ctx * channels, channels)], r_ref.at[:, :, pl.ds(ctx * block, block)], local.at[1]
        ),
    ]
    for copy in copies + own:
        copy.start()
    for copy in copies + own:
        copy.wait()


def gather_kernel(ctx_count, chan_count, y_ref, o_ref, send, recv, local):
    ctx, chan = lax.axis_index("ctx"), lax.axis_index("chan")
    me = ctx * chan_count + chan
    total = ctx_count * chan_count
    pairs, rows = y_ref.shape[0], o_ref.shape[1]
    slot = pl.ds((chan * ctx_count + ctx) * pairs, pairs)
    greet_all(ctx_count, chan_count, me)
    copies = []
    for offset in range(1, total):
        other = lax.rem(me + offset, total)
        copies.append(
            pltpu.make_async_remote_copy(
                src_ref=y_ref.at[:, pl.ds(other * rows, rows)],
                dst_ref=o_ref.at[slot],
                send_sem=send.at[offset - 1],
                recv_sem=recv.at[offset - 1],
                device_id=(other // chan_count, lax.rem(other, chan_count)),
                device_id_type=MESH,
            )
        )
    copies.append(pltpu.make_async_copy(y_ref.at[:, pl.ds(me * rows, rows)], o_ref.at[slot], local.at[0]))
    for copy in copies:
        copy.start()
    for copy in copies:
        copy.wait()


def dot(a, b):
    return jnp.dot(a, b, preferred_element_type=jnp.float32)


def convolve_kernel(x_ref, r_ref, w1_ref, w2_ref, w3_ref, v1_ref, tw_ref, y_ref, g_ref):
    rows_total = x_ref.shape[1]
    chunk = 128

    @pl.loop(0, x_ref.shape[0])
    def _(pair):
        x = x_ref.at[pair]

        @pl.loop(0, rows_total // chunk)
        def _(step):
            at = pl.ds(pl.multiple_of(step * chunk, chunk), chunk)
            below = pl.ds(pl.multiple_of(rows_total + step * chunk, chunk), chunk)
            real, imag = dot(w1_ref[0, at], x[...]), dot(w1_ref[1, at], x[...])
            t_real, t_imag = tw_ref[0, at], tw_ref[1, at]
            for which in range(2):
                cols = slice(which * lanes, (which + 1) * lanes)
                a_real, a_imag = real[:, cols], imag[:, cols]
                turned = jnp.concatenate(
                    [a_real * t_real - a_imag * t_imag, a_real * t_imag + a_imag * t_real], axis=1
                )
                bins = dot(turned.astype(jnp.bfloat16), w2_ref[...])
                b_real, b_imag = bins[:, :lanes], bins[:, lanes:]
                f_real = r_ref[0, 2 * pair + which, at].astype(jnp.float32)
                f_imag = r_ref[1, 2 * pair + which, at].astype(jnp.float32)
                shaped = jnp.concatenate(
                    [b_real * f_real - b_imag * f_imag, b_real * f_imag + b_imag * f_real], axis=1
                )
                back = dot(shaped.astype(jnp.bfloat16), w3_ref[...])
                z_real, z_imag = back[:, :lanes], back[:, lanes:]
                g_ref[at, cols] = (z_real * t_real + z_imag * t_imag).astype(jnp.bfloat16)
                g_ref[below, cols] = (z_imag * t_real - z_real * t_imag).astype(jnp.bfloat16)

        @pl.loop(0, rows_total // chunk)
        def _(step):
            at = pl.ds(pl.multiple_of(step * chunk, chunk), chunk)
            y_ref[pair, at] = dot(v1_ref[at], g_ref[...]).astype(jnp.bfloat16)


def channel_body(value_branch, key_branch, gate_branch, skip_gain, spectra):
    channels, tokens = value_branch.shape
    ctx_count, chan_count = lax.axis_size("ctx"), lax.axis_size("chan")
    total = ctx_count * chan_count
    rows = tokens // lanes
    rows_total = rows * total
    pairs = channels // total // 2
    carried = (key_branch.astype(jnp.float32) * value_branch.astype(jnp.float32)).astype(jnp.bfloat16)
    paired = carried.reshape(channels // 2, 2, rows, lanes).swapaxes(1, 2).reshape(channels // 2, rows, 2 * lanes)
    local_channels = spectra.shape[1]
    block = spectra.shape[3] // lanes
    turned = turn_spectra(spectra.reshape(2 * local_channels, block, lanes))
    turned = turned.reshape(2, local_channels, block, lanes)
    sems = lambda count: pltpu.SemaphoreType.DMA((count,))
    series, response = pl.pallas_call(
        functools.partial(spread_kernel, ctx_count, chan_count),
        in_specs=[VMEM, VMEM],
        out_specs=[VMEM, VMEM],
        out_shape=[
            jax.ShapeDtypeStruct((pairs, rows_total, 2 * lanes), jnp.bfloat16),
            jax.ShapeDtypeStruct((2, 2 * pairs, rows_total, lanes), jnp.bfloat16),
        ],
        scratch_shapes=[sems(total - 1), sems(total - 1), sems(ctx_count - 1), sems(ctx_count - 1), sems(2)],
        compiler_params=pltpu.CompilerParams(collective_id=0, has_side_effects=True),
    )(paired, turned)
    tables = [jnp.asarray(t) for t in transform_tables(rows_total, ctx_count)]
    convolved = pl.pallas_call(
        convolve_kernel,
        in_specs=[VMEM] * 7,
        out_specs=VMEM,
        out_shape=jax.ShapeDtypeStruct((pairs, rows_total, 2 * lanes), jnp.bfloat16),
        scratch_shapes=[pltpu.VMEM((2 * rows_total, 2 * lanes), jnp.bfloat16)],
    )(series, response, *tables)
    gathered = pl.pallas_call(
        functools.partial(gather_kernel, ctx_count, chan_count),
        in_specs=[VMEM],
        out_specs=VMEM,
        out_shape=jax.ShapeDtypeStruct((channels // 2, rows, 2 * lanes), jnp.bfloat16),
        scratch_shapes=[sems(total - 1), sems(total - 1), sems(1)],
        compiler_params=pltpu.CompilerParams(collective_id=1, has_side_effects=True),
    )(convolved)
    tokens_conv = gathered.reshape(channels // 2, rows, 2, lanes).swapaxes(1, 2).reshape(channels, tokens)
    result = gate_branch.astype(jnp.float32) * (
        tokens_conv.astype(jnp.float32) + skip_gain[:, None] * carried.astype(jnp.float32)
    )
    return result.astype(jnp.bfloat16)


def body(value_branch, key_branch, gate_branch, skip_gain, spectra):
    channels, tokens = value_branch.shape
    ctx_count, chan_count = lax.axis_size("ctx"), lax.axis_size("chan")
    total = ctx_count * chan_count
    block_rows = tokens * chan_count // lanes
    fits = (
        channels % (2 * total) == 0
        and tokens % (16 * lanes) == 0
        and block_rows <= lanes
        and lanes % block_rows == 0
        and 2 * spectra.shape[1] % 16 == 0
        and (tokens * total // lanes) % lanes == 0
    )
    chosen = channel_body if fits else blockwise_body
    return chosen(value_branch, key_branch, gate_branch, skip_gain, spectra)


def solution(mesh):
    in_specs = (
        P(None, ("ctx", "chan")),
        P(None, ("ctx", "chan")),
        P(None, ("ctx", "chan")),
        P(),
        P(None, "chan", "ctx", None),
    )
    out_specs = P(None, ("ctx", "chan"))
    return jax.shard_map(body, mesh=mesh, in_specs=in_specs, out_specs=out_specs, check_vma=False)
```

```python
import functools
import math

import jax
import jax.numpy as jnp
import numpy as np
from jax import lax
from jax.experimental import pallas as pl
from jax.experimental.pallas import tpu as pltpu
from jax.sharding import PartitionSpec as P

two_pi = 2.0 * math.pi
first_factor = 128
highest = lax.Precision.HIGHEST


def reversed_bits(numbers, bit_count):
    result = numbers * 0
    for bit_number in range(bit_count):
        result = result + (numbers >> bit_number & 1) * (1 << bit_count - 1 - bit_number)
    return result


def phase_pair(radians):
    return (jnp.cos(radians), jnp.sin(radians))


def block_table(length_of, direction):
    counter = jnp.arange(length_of, dtype=jnp.int32)
    product = counter[:, None] * counter[None, :] % length_of
    cosine, sine = phase_pair(direction * two_pi / length_of * product.astype(jnp.float32))
    upper_rows = jnp.stack([cosine, -sine], axis=1)
    lower_rows = jnp.stack([sine, cosine], axis=1)
    return jnp.stack([upper_rows, lower_rows], axis=0)


def complex_mul(signal, factor):
    factor_real, factor_imag = factor
    return jnp.stack(
        [
            signal[0] * factor_real - signal[1] * factor_imag,
            signal[0] * factor_imag + signal[1] * factor_real,
        ]
    )


def forward_local(signal):
    channel_count, seq_length = (signal.shape[1], signal.shape[2])
    second_factor = seq_length // first_factor
    blocked = signal.reshape(2, channel_count, first_factor, second_factor)
    section_one = jnp.einsum(
        "orca,cxaq->oxrq", block_table(first_factor, -1.0), blocked, precision=highest
    )
    column = jnp.arange(first_factor, dtype=jnp.int32)[:, None]
    within = jnp.arange(second_factor, dtype=jnp.int32)[None, :]
    twiddle = phase_pair(-two_pi / seq_length * (column * within).astype(jnp.float32))
    section_two = complex_mul(section_one, twiddle)
    section_three = jnp.einsum(
        "peoq,oxrq->pxer", block_table(second_factor, -1.0), section_two, precision=highest
    )
    return section_three.reshape(2, channel_count, seq_length)


def inverse_local(signal):
    channel_count, seq_length = (signal.shape[1], signal.shape[2])
    second_factor = seq_length // first_factor
    blocked = signal.reshape(2, channel_count, second_factor, first_factor)
    section_one = jnp.einsum(
        "pqoe,oxer->pxqr", block_table(second_factor, 1.0), blocked, precision=highest
    )
    within = jnp.arange(second_factor, dtype=jnp.int32)[:, None]
    column = jnp.arange(first_factor, dtype=jnp.int32)[None, :]
    twiddle = phase_pair(two_pi / seq_length * (within * column).astype(jnp.float32))
    section_two = complex_mul(section_one, twiddle)
    section_three = jnp.einsum(
        "paor,oxqr->pxaq", block_table(first_factor, 1.0), section_two, precision=highest
    )
    return section_three.reshape(2, channel_count, seq_length)


def blockwise_body(value_branch, key_branch, gate_branch, skip_gain, spectra):
    carried = (key_branch.astype(jnp.float32) * value_branch.astype(jnp.float32)).astype(
        jnp.bfloat16
    )
    series = lax.all_to_all(carried, "chan", split_axis=0, concat_axis=1, tiled=True)
    channel_count, seq_length = series.shape
    ctx_count = lax.axis_size("ctx")
    bit_count = ctx_count.bit_length() - 1
    device = lax.axis_index("ctx")
    total_length = seq_length * ctx_count
    counter = jnp.arange(ctx_count, dtype=jnp.int32)
    target = reversed_bits(counter, bit_count)
    blocks = lax.all_to_all(
        series.reshape(channel_count, 1, seq_length), "ctx", split_axis=2, concat_axis=1, tiled=True
    )
    matrix = jnp.stack(
        phase_pair(
            -two_pi
            / ctx_count
            * (target[:, None] * counter[None, :] % ctx_count).astype(jnp.float32)
        )
    )
    rows = jnp.einsum("ojp,xps->oxjs", matrix, blocks.astype(jnp.float32), precision=highest)
    received = lax.all_to_all(rows, "ctx", split_axis=2, concat_axis=3, tiled=True)
    signal = received.reshape(2, channel_count, seq_length)
    device_rank = reversed_bits(device, bit_count)
    positions = jnp.arange(seq_length, dtype=jnp.int32)
    radians = two_pi / total_length * (positions * device_rank).astype(jnp.float32)
    signal = complex_mul(signal, phase_pair(-radians))
    spectrum = forward_local(signal)
    shaped = complex_mul(spectrum, (spectra[0, :, 0, :], spectra[1, :, 0, :]))
    returned = complex_mul(inverse_local(shaped), phase_pair(radians))
    parts = lax.all_to_all(
        returned.reshape(2, channel_count, 1, seq_length),
        "ctx",
        split_axis=3,
        concat_axis=2,
        tiled=True,
    )
    cosine, sine = phase_pair(
        two_pi / ctx_count * (counter[:, None] * target[None, :] % ctx_count).astype(jnp.float32)
    )
    matrix = jnp.stack([cosine, -sine])
    summed = jnp.einsum("opj,oxjs->xps", matrix, parts, precision=highest) / total_length
    local_conv = summed.astype(jnp.bfloat16)
    convolved = lax.all_to_all(local_conv, "ctx", split_axis=1, concat_axis=2, tiled=True).reshape(
        channel_count, seq_length
    )
    tokens_conv = lax.all_to_all(convolved, "chan", split_axis=1, concat_axis=0, tiled=True)
    result = gate_branch.astype(jnp.float32) * (
        tokens_conv.astype(jnp.float32) + skip_gain[:, None] * carried.astype(jnp.float32)
    )
    return result.astype(jnp.bfloat16)


lanes = 128
MESH = pl.DeviceIdType.MESH
VMEM = pl.BlockSpec(memory_space=pltpu.VMEM)


@functools.lru_cache(maxsize=None)
def transform_tables(rows_total, ctx_count):
    length = rows_total * lanes
    bit_count = ctx_count.bit_length() - 1
    rev = np.array([int(format(j, "b").zfill(bit_count)[::-1], 2) if bit_count else 0 for j in range(ctx_count)])
    a = np.arange(rows_total // ctx_count)
    k1 = (rev[:, None] + ctx_count * a[None, :]).reshape(-1)
    fold = lanes // (rows_total // ctx_count)
    k2 = np.arange(lanes).reshape(lanes // fold, fold).T.reshape(-1)
    n1, n2 = np.arange(rows_total), np.arange(lanes)
    f1 = np.exp(-2j * np.pi * (np.outer(k1, n1) % rows_total) / rows_total)
    f2 = np.exp(-2j * np.pi * (np.outer(n2, k2) % lanes) / lanes)
    tw = np.exp(-2j * np.pi * (np.outer(k1, n2) % length) / length)
    w1 = np.stack([f1.real, f1.imag])
    w2 = np.block([[f2.real, f2.imag], [-f2.imag, f2.real]])
    b2 = f2.conj().T
    w3 = np.block([[b2.real, b2.imag], [-b2.imag, b2.real]])
    b1 = f1.conj().T / length
    v1 = np.concatenate([b1.real, -b1.imag], axis=1)
    half = lambda t: np.asarray(t, dtype=jnp.bfloat16)
    return half(w1), half(w2), half(w3), half(v1), np.stack([tw.real, tw.imag]).astype(np.float32)


def greet_all(ctx_count, chan_count, me):
    total = ctx_count * chan_count
    barrier = pltpu.get_barrier_semaphore()

    @pl.loop(1, total)
    def _(offset):
        other = lax.rem(me + offset, total)
        pl.semaphore_signal(
            barrier, inc=1, device_id=(other // chan_count, lax.rem(other, chan_count)), device_id_type=MESH
        )

    pl.semaphore_wait(barrier, total - 1)


def dot(a, b):
    return jnp.dot(a, b, preferred_element_type=jnp.float32)


def fused_kernel(
    ctx_count, chan_count, c_ref, s_hbm, *refs
):
    tables_hbm, (o_ref,), tables = refs[:5], refs[5:6], refs[6:11]
    w1_ref, w2_ref, w3_ref, v1_ref, tw_ref = tables
    s_ref, stage, r_ref, x_ref, y_ref, g_ref = refs[11:17]
    send_c, recv_c, send_s, recv_s, send_y, recv_y, local = refs[17:]
    ctx, chan = lax.axis_index("ctx"), lax.axis_index("chan")
    me = ctx * chan_count + chan
    total = ctx_count * chan_count
    pairs, rows = x_ref.shape[0], c_ref.shape[1]
    rows_total = x_ref.shape[1]
    block = stage.shape[2]
    local_channels = stage.shape[1]

    loads = [pltpu.make_async_copy(s_hbm, s_ref, local.at[0])]
    for i, (source, target) in enumerate(zip(tables_hbm, tables)):
        loads.append(pltpu.make_async_copy(source, target, local.at[1 + i]))
    for load in loads:
        load.start()
    greet_all(ctx_count, chan_count, me)

    def place(offset):
        other = lax.rem(me + offset, total)
        return other, other // chan_count, lax.rem(other, chan_count)

    def slot(ctx_index, chan_index):
        return (chan_index * ctx_count + ctx_index) * pairs

    my_rows = pl.ds(pl.multiple_of(me * rows, rows), rows)
    my_block = pl.ds(pl.multiple_of(ctx * block, block), block)

    def carried_copy(pair, offset):
        other, other_ctx, other_chan = place(offset)
        return pltpu.make_async_remote_copy(
            src_ref=c_ref.at[slot(other_ctx, other_chan) + pair],
            dst_ref=x_ref.at[pair, my_rows],
            send_sem=send_c.at[pair, offset - 1],
            recv_sem=recv_c.at[pair, offset - 1],
            device_id=(other_ctx, other_chan),
            device_id_type=MESH,
        )

    def spectra_copy(pair, offset):
        other_ctx = lax.rem(ctx + offset, ctx_count)
        return pltpu.make_async_remote_copy(
            src_ref=stage.at[:, pl.ds((other_ctx * pairs + pair) * 2, 2)],
            dst_ref=r_ref.at[:, pl.ds(2 * pair, 2), my_block],
            send_sem=send_s.at[pair, offset - 1],
            recv_sem=recv_s.at[pair, offset - 1],
            device_id=(other_ctx, chan),
            device_id_type=MESH,
        )

    def result_copy(pair, offset):
        other, other_ctx, other_chan = place(offset)
        return pltpu.make_async_remote_copy(
            src_ref=y_ref.at[pair, pl.ds(pl.multiple_of(other * rows, rows), rows)],
            dst_ref=o_ref.at[slot(ctx, chan) + pair],
            send_sem=send_y.at[pair, offset - 1],
            recv_sem=recv_y.at[pair, offset - 1],
            device_id=(other_ctx, other_chan),
            device_id_type=MESH,
        )

    def each(copy_of, pair, count, act):
        @pl.loop(1, count)
        def _(offset):
            act(copy_of(pair, offset))

    def turned(part, channel):
        flipped = s_ref[part * local_channels + channel].T
        pieces = [flipped[f * block : (f + 1) * block] for f in range(flipped.shape[0] // block)]
        return jnp.concatenate(pieces, axis=1).astype(jnp.bfloat16)

    start = lambda copy: copy.start()
    for pair in range(pairs):
        each(carried_copy, pair, total, start)
        if pair == 0:
            loads[0].wait()

        @pl.loop(1, ctx_count)
        def _(offset):
            first = (lax.rem(ctx + offset, ctx_count) * pairs + pair) * 2
            for part in range(2):
                for which in range(2):
                    stage[part, first + which] = turned(part, first + which)

        for part in range(2):
            for which in range(2):
                r_ref[part, 2 * pair + which, my_block] = turned(part, (ctx * pairs + pair) * 2 + which)
        x_ref[pair, my_rows] = c_ref[slot(ctx, chan) + pair]
        each(spectra_copy, pair, ctx_count, start)

    for load in loads[1:]:
        load.wait()
    chunk = 128
    for pair in range(pairs):
        each(carried_copy, pair, total, lambda copy: copy.wait_recv())
        each(spectra_copy, pair, ctx_count, lambda copy: copy.wait_recv())
        x = x_ref.at[pair]

        @pl.loop(0, rows_total // chunk)
        def _(step):
            at = pl.ds(pl.multiple_of(step * chunk, chunk), chunk)
            below = pl.ds(pl.multiple_of(rows_total + step * chunk, chunk), chunk)
            real, imag = dot(w1_ref[0, at], x[...]), dot(w1_ref[1, at], x[...])
            t_real, t_imag = tw_ref[0, at], tw_ref[1, at]
            for which in range(2):
                cols = slice(which * lanes, (which + 1) * lanes)
                a_real, a_imag = real[:, cols], imag[:, cols]
                twiddled = jnp.concatenate(
                    [a_real * t_real - a_imag * t_imag, a_real * t_imag + a_imag * t_real], axis=1
                )
                bins = dot(twiddled.astype(jnp.bfloat16), w2_ref[...])
                b_real, b_imag = bins[:, :lanes], bins[:, lanes:]
                f_real = r_ref[0, 2 * pair + which, at].astype(jnp.float32)
                f_imag = r_ref[1, 2 * pair + which, at].astype(jnp.float32)
                shaped = jnp.concatenate(
                    [b_real * f_real - b_imag * f_imag, b_real * f_imag + b_imag * f_real], axis=1
                )
                back = dot(shaped.astype(jnp.bfloat16), w3_ref[...])
                z_real, z_imag = back[:, :lanes], back[:, lanes:]
                g_ref[at, cols] = (z_real * t_real + z_imag * t_imag).astype(jnp.bfloat16)
                g_ref[below, cols] = (z_imag * t_real - z_real * t_imag).astype(jnp.bfloat16)

        @pl.loop(0, rows_total // chunk)
        def _(step):
            at = pl.ds(pl.multiple_of(step * chunk, chunk), chunk)
            y_ref[pair, at] = dot(v1_ref[at], g_ref[...]).astype(jnp.bfloat16)

        o_ref[slot(ctx, chan) + pair] = y_ref[pair, my_rows]
        each(result_copy, pair, total, start)

    for pair in range(pairs):
        each(carried_copy, pair, total, lambda copy: copy.wait_send())
        each(spectra_copy, pair, ctx_count, lambda copy: copy.wait_send())
        each(result_copy, pair, total, lambda copy: copy.wait())


def channel_body(value_branch, key_branch, gate_branch, skip_gain, spectra):
    channels, tokens = value_branch.shape
    ctx_count, chan_count = lax.axis_size("ctx"), lax.axis_size("chan")
    total = ctx_count * chan_count
    rows = tokens // lanes
    rows_total = rows * total
    pairs = channels // total // 2
    carried = (key_branch.astype(jnp.float32) * value_branch.astype(jnp.float32)).astype(jnp.bfloat16)
    paired = carried.reshape(channels // 2, 2, rows, lanes).swapaxes(1, 2).reshape(channels // 2, rows, 2 * lanes)
    local_channels = spectra.shape[1]
    block = spectra.shape[3] // lanes
    tables = [jnp.asarray(t) for t in transform_tables(rows_total, ctx_count)]
    sems = lambda *shape: pltpu.SemaphoreType.DMA(shape)
    hbm = pl.BlockSpec(memory_space=pl.ANY)
    gathered = pl.pallas_call(
        functools.partial(fused_kernel, ctx_count, chan_count),
        in_specs=[VMEM] + [hbm] * 6,
        out_specs=VMEM,
        out_shape=jax.ShapeDtypeStruct((channels // 2, rows, 2 * lanes), jnp.bfloat16),
        scratch_shapes=[pltpu.VMEM(t.shape, t.dtype) for t in tables]
        + [
            pltpu.VMEM((2 * local_channels, block, lanes), jnp.float32),
            pltpu.VMEM((2, local_channels, block, lanes), jnp.bfloat16),
            pltpu.VMEM((2, 2 * pairs, rows_total, lanes), jnp.bfloat16),
            pltpu.VMEM((pairs, rows_total, 2 * lanes), jnp.bfloat16),
            pltpu.VMEM((pairs, rows_total, 2 * lanes), jnp.bfloat16),
            pltpu.VMEM((2 * rows_total, 2 * lanes), jnp.bfloat16),
        ]
        + [sems(pairs, count - 1) for count in (total, total, ctx_count, ctx_count, total, total)]
        + [sems(6)],
        compiler_params=pltpu.CompilerParams(collective_id=0, has_side_effects=True),
    )(paired, spectra.reshape(2 * local_channels, block, lanes), *tables)
    tokens_conv = gathered.reshape(channels // 2, rows, 2, lanes).swapaxes(1, 2).reshape(channels, tokens)
    result = gate_branch.astype(jnp.float32) * (
        tokens_conv.astype(jnp.float32) + skip_gain[:, None] * carried.astype(jnp.float32)
    )
    return result.astype(jnp.bfloat16)


def body(value_branch, key_branch, gate_branch, skip_gain, spectra):
    channels, tokens = value_branch.shape
    ctx_count, chan_count = lax.axis_size("ctx"), lax.axis_size("chan")
    total = ctx_count * chan_count
    block_rows = tokens * chan_count // lanes
    fits = (
        channels % (2 * total) == 0
        and tokens % (16 * lanes) == 0
        and block_rows <= lanes
        and lanes % block_rows == 0
        and (tokens * total // lanes) % lanes == 0
    )
    chosen = channel_body if fits else blockwise_body
    return chosen(value_branch, key_branch, gate_branch, skip_gain, spectra)


def solution(mesh):
    in_specs = (
        P(None, ("ctx", "chan")),
        P(None, ("ctx", "chan")),
        P(None, ("ctx", "chan")),
        P(),
        P(None, "chan", "ctx", None),
    )
    out_specs = P(None, ("ctx", "chan"))
    return jax.shard_map(body, mesh=mesh, in_specs=in_specs, out_specs=out_specs, check_vma=False)
```

```python
import functools
import math

import jax
import jax.numpy as jnp
import numpy as np
from jax import lax
from jax.experimental import pallas as pl
from jax.experimental.pallas import tpu as pltpu
from jax.sharding import PartitionSpec as P

two_pi = 2.0 * math.pi
first_factor = 128
highest = lax.Precision.HIGHEST


def reversed_bits(numbers, bit_count):
    result = numbers * 0
    for bit_number in range(bit_count):
        result = result + (numbers >> bit_number & 1) * (1 << bit_count - 1 - bit_number)
    return result


def phase_pair(radians):
    return (jnp.cos(radians), jnp.sin(radians))


def block_table(length_of, direction):
    counter = jnp.arange(length_of, dtype=jnp.int32)
    product = counter[:, None] * counter[None, :] % length_of
    cosine, sine = phase_pair(direction * two_pi / length_of * product.astype(jnp.float32))
    upper_rows = jnp.stack([cosine, -sine], axis=1)
    lower_rows = jnp.stack([sine, cosine], axis=1)
    return jnp.stack([upper_rows, lower_rows], axis=0)


def complex_mul(signal, factor):
    factor_real, factor_imag = factor
    return jnp.stack(
        [
            signal[0] * factor_real - signal[1] * factor_imag,
            signal[0] * factor_imag + signal[1] * factor_real,
        ]
    )


def forward_local(signal):
    channel_count, seq_length = (signal.shape[1], signal.shape[2])
    second_factor = seq_length // first_factor
    blocked = signal.reshape(2, channel_count, first_factor, second_factor)
    section_one = jnp.einsum(
        "orca,cxaq->oxrq", block_table(first_factor, -1.0), blocked, precision=highest
    )
    column = jnp.arange(first_factor, dtype=jnp.int32)[:, None]
    within = jnp.arange(second_factor, dtype=jnp.int32)[None, :]
    twiddle = phase_pair(-two_pi / seq_length * (column * within).astype(jnp.float32))
    section_two = complex_mul(section_one, twiddle)
    section_three = jnp.einsum(
        "peoq,oxrq->pxer", block_table(second_factor, -1.0), section_two, precision=highest
    )
    return section_three.reshape(2, channel_count, seq_length)


def inverse_local(signal):
    channel_count, seq_length = (signal.shape[1], signal.shape[2])
    second_factor = seq_length // first_factor
    blocked = signal.reshape(2, channel_count, second_factor, first_factor)
    section_one = jnp.einsum(
        "pqoe,oxer->pxqr", block_table(second_factor, 1.0), blocked, precision=highest
    )
    within = jnp.arange(second_factor, dtype=jnp.int32)[:, None]
    column = jnp.arange(first_factor, dtype=jnp.int32)[None, :]
    twiddle = phase_pair(two_pi / seq_length * (within * column).astype(jnp.float32))
    section_two = complex_mul(section_one, twiddle)
    section_three = jnp.einsum(
        "paor,oxqr->pxaq", block_table(first_factor, 1.0), section_two, precision=highest
    )
    return section_three.reshape(2, channel_count, seq_length)


def blockwise_body(value_branch, key_branch, gate_branch, skip_gain, spectra):
    carried = (key_branch.astype(jnp.float32) * value_branch.astype(jnp.float32)).astype(
        jnp.bfloat16
    )
    series = lax.all_to_all(carried, "chan", split_axis=0, concat_axis=1, tiled=True)
    channel_count, seq_length = series.shape
    ctx_count = lax.axis_size("ctx")
    bit_count = ctx_count.bit_length() - 1
    device = lax.axis_index("ctx")
    total_length = seq_length * ctx_count
    counter = jnp.arange(ctx_count, dtype=jnp.int32)
    target = reversed_bits(counter, bit_count)
    blocks = lax.all_to_all(
        series.reshape(channel_count, 1, seq_length), "ctx", split_axis=2, concat_axis=1, tiled=True
    )
    matrix = jnp.stack(
        phase_pair(
            -two_pi
            / ctx_count
            * (target[:, None] * counter[None, :] % ctx_count).astype(jnp.float32)
        )
    )
    rows = jnp.einsum("ojp,xps->oxjs", matrix, blocks.astype(jnp.float32), precision=highest)
    received = lax.all_to_all(rows, "ctx", split_axis=2, concat_axis=3, tiled=True)
    signal = received.reshape(2, channel_count, seq_length)
    device_rank = reversed_bits(device, bit_count)
    positions = jnp.arange(seq_length, dtype=jnp.int32)
    radians = two_pi / total_length * (positions * device_rank).astype(jnp.float32)
    signal = complex_mul(signal, phase_pair(-radians))
    spectrum = forward_local(signal)
    shaped = complex_mul(spectrum, (spectra[0, :, 0, :], spectra[1, :, 0, :]))
    returned = complex_mul(inverse_local(shaped), phase_pair(radians))
    parts = lax.all_to_all(
        returned.reshape(2, channel_count, 1, seq_length),
        "ctx",
        split_axis=3,
        concat_axis=2,
        tiled=True,
    )
    cosine, sine = phase_pair(
        two_pi / ctx_count * (counter[:, None] * target[None, :] % ctx_count).astype(jnp.float32)
    )
    matrix = jnp.stack([cosine, -sine])
    summed = jnp.einsum("opj,oxjs->xps", matrix, parts, precision=highest) / total_length
    local_conv = summed.astype(jnp.bfloat16)
    convolved = lax.all_to_all(local_conv, "ctx", split_axis=1, concat_axis=2, tiled=True).reshape(
        channel_count, seq_length
    )
    tokens_conv = lax.all_to_all(convolved, "chan", split_axis=1, concat_axis=0, tiled=True)
    result = gate_branch.astype(jnp.float32) * (
        tokens_conv.astype(jnp.float32) + skip_gain[:, None] * carried.astype(jnp.float32)
    )
    return result.astype(jnp.bfloat16)


lanes = 128
MESH = pl.DeviceIdType.MESH
VMEM = pl.BlockSpec(memory_space=pltpu.VMEM)


@functools.lru_cache(maxsize=None)
def transform_tables(rows_total, ctx_count):
    length = rows_total * lanes
    bit_count = ctx_count.bit_length() - 1
    rev = np.array([int(format(j, "b").zfill(bit_count)[::-1], 2) if bit_count else 0 for j in range(ctx_count)])
    a = np.arange(rows_total // ctx_count)
    k1 = (rev[:, None] + ctx_count * a[None, :]).reshape(-1)
    fold = lanes // (rows_total // ctx_count)
    k2 = np.arange(lanes).reshape(lanes // fold, fold).T.reshape(-1)
    n1, n2 = np.arange(rows_total), np.arange(lanes)
    f1 = np.exp(-2j * np.pi * (np.outer(k1, n1) % rows_total) / rows_total)
    f2 = np.exp(-2j * np.pi * (np.outer(n2, k2) % lanes) / lanes)
    tw = np.exp(-2j * np.pi * (np.outer(k1, n2) % length) / length)
    w1 = np.stack([f1.real, f1.imag])
    w2 = np.block([[f2.real, f2.imag], [-f2.imag, f2.real]])
    b2 = f2.conj().T
    w3 = np.block([[b2.real, b2.imag], [-b2.imag, b2.real]])
    b1 = f1.conj().T / length
    v1 = np.concatenate([b1.real, -b1.imag], axis=1)
    half = lambda t: np.asarray(t, dtype=jnp.bfloat16)
    return half(w1), half(w2), half(w3), half(v1), np.stack([tw.real, tw.imag]).astype(np.float32)


def greet_all(ctx_count, chan_count, me):
    total = ctx_count * chan_count
    barrier = pltpu.get_barrier_semaphore()

    @pl.loop(1, total)
    def _(offset):
        other = lax.rem(me + offset, total)
        pl.semaphore_signal(
            barrier, inc=1, device_id=(other // chan_count, lax.rem(other, chan_count)), device_id_type=MESH
        )


def dot(a, b):
    return jnp.dot(a, b, preferred_element_type=jnp.float32)


def fused_kernel(ctx_count, chan_count, skip_ref, v_hbm, k_hbm, gate_hbm, s_hbm, *refs):
    tables_hbm, (out_ref,), tables = refs[:5], refs[5:6], refs[6:11]
    w1_ref, w2_ref, w3_ref, v1_ref, tw_ref = tables
    s_ref, stage, r_ref, x_ref, y_ref, g_ref = refs[11:17]
    v_ref, k_ref, gate_ref, c_ref, o_ref = refs[17:22]
    send_c, recv_c, send_s, recv_s, send_y, recv_y, local = refs[22:]
    ctx, chan = lax.axis_index("ctx"), lax.axis_index("chan")
    me = ctx * chan_count + chan
    total = ctx_count * chan_count
    pairs, rows = x_ref.shape[0], c_ref.shape[1]
    rows_total = x_ref.shape[1]
    block = stage.shape[2]
    local_channels = stage.shape[1]

    greet_all(ctx_count, chan_count, me)
    sources = (v_hbm, k_hbm, s_hbm, gate_hbm, *tables_hbm)
    targets = (v_ref, k_ref, s_ref, gate_ref, *tables)
    loads = [
        pltpu.make_async_copy(source, target, local.at[i]) for i, (source, target) in enumerate(zip(sources, targets))
    ]
    for load in loads:
        load.start()
    group = 2 * ctx_count
    loads[0].wait()
    loads[1].wait()

    @pl.loop(0, v_ref.shape[0] // group)
    def _(index):
        at = pl.ds(pl.multiple_of(index * group, group), group)
        product = (k_ref[at].astype(jnp.float32) * v_ref[at].astype(jnp.float32)).astype(jnp.bfloat16)
        split = product.astype(jnp.float32).reshape(ctx_count, 2, rows, lanes)
        packed = jnp.concatenate([split[:, 0], split[:, 1]], axis=2)
        c_ref[pl.ds(index * ctx_count, ctx_count)] = packed.astype(jnp.bfloat16)

    pl.semaphore_wait(pltpu.get_barrier_semaphore(), total - 1)

    def place(offset):
        other = lax.rem(me + offset, total)
        return other, other // chan_count, lax.rem(other, chan_count)

    def slot(ctx_index, chan_index, pair):
        return (chan_index * pairs + pair) * ctx_count + ctx_index

    my_rows = pl.ds(pl.multiple_of(me * rows, rows), rows)
    my_block = pl.ds(pl.multiple_of(ctx * block, block), block)

    def carried_copy(pair, offset):
        other, other_ctx, other_chan = place(offset)
        return pltpu.make_async_remote_copy(
            src_ref=c_ref.at[slot(other_ctx, other_chan, pair)],
            dst_ref=x_ref.at[pair, my_rows],
            send_sem=send_c.at[pair, offset - 1],
            recv_sem=recv_c.at[pair, offset - 1],
            device_id=(other_ctx, other_chan),
            device_id_type=MESH,
        )

    def spectra_copy(pair, offset):
        other_ctx = lax.rem(ctx + offset, ctx_count)
        return pltpu.make_async_remote_copy(
            src_ref=stage.at[:, pl.ds((pair * ctx_count + other_ctx) * 2, 2)],
            dst_ref=r_ref.at[:, pl.ds(2 * pair, 2), my_block],
            send_sem=send_s.at[pair, offset - 1],
            recv_sem=recv_s.at[pair, offset - 1],
            device_id=(other_ctx, chan),
            device_id_type=MESH,
        )

    def result_copy(pair, offset):
        other, other_ctx, other_chan = place(offset)
        return pltpu.make_async_remote_copy(
            src_ref=y_ref.at[pair, pl.ds(pl.multiple_of(other * rows, rows), rows)],
            dst_ref=o_ref.at[slot(ctx, chan, pair)],
            send_sem=send_y.at[pair, offset - 1],
            recv_sem=recv_y.at[pair, offset - 1],
            device_id=(other_ctx, other_chan),
            device_id_type=MESH,
        )

    def each(copy_of, pair, count, act):
        @pl.loop(1, count)
        def _(offset):
            act(copy_of(pair, offset))

    def turned(part, channel):
        flipped = s_ref[part * local_channels + channel].T
        pieces = [flipped[f * block : (f + 1) * block] for f in range(flipped.shape[0] // block)]
        return jnp.concatenate(pieces, axis=1).astype(jnp.bfloat16)

    start = lambda copy: copy.start()
    for pair in range(pairs):
        each(carried_copy, pair, total, start)
        if pair == 0:
            loads[2].wait()

        @pl.loop(1, ctx_count)
        def _(offset):
            first = (pair * ctx_count + lax.rem(ctx + offset, ctx_count)) * 2
            for part in range(2):
                for which in range(2):
                    stage[part, first + which] = turned(part, first + which)

        for part in range(2):
            for which in range(2):
                r_ref[part, 2 * pair + which, my_block] = turned(part, (pair * ctx_count + ctx) * 2 + which)
        x_ref[pair, my_rows] = c_ref[slot(ctx, chan, pair)]
        each(spectra_copy, pair, ctx_count, start)

    for load in loads[3:]:
        load.wait()
    chunk = 2 * lanes
    for pair in range(pairs):
        each(carried_copy, pair, total, lambda copy: copy.wait_recv())
        each(spectra_copy, pair, ctx_count, lambda copy: copy.wait_recv())
        x = x_ref.at[pair]

        @pl.loop(0, rows_total // chunk)
        def _(step):
            at = pl.ds(pl.multiple_of(step * chunk, chunk), chunk)
            below = pl.ds(pl.multiple_of(rows_total + step * chunk, chunk), chunk)
            real, imag = dot(w1_ref[0, at], x[...]), dot(w1_ref[1, at], x[...])
            t_real, t_imag = tw_ref[0, at], tw_ref[1, at]
            for which in range(2):
                cols = slice(which * lanes, (which + 1) * lanes)
                a_real, a_imag = real[:, cols], imag[:, cols]
                twiddled = jnp.concatenate(
                    [a_real * t_real - a_imag * t_imag, a_real * t_imag + a_imag * t_real], axis=1
                )
                bins = dot(twiddled.astype(jnp.bfloat16), w2_ref[...])
                b_real, b_imag = bins[:, :lanes], bins[:, lanes:]
                f_real = r_ref[0, 2 * pair + which, at].astype(jnp.float32)
                f_imag = r_ref[1, 2 * pair + which, at].astype(jnp.float32)
                shaped = jnp.concatenate(
                    [b_real * f_real - b_imag * f_imag, b_real * f_imag + b_imag * f_real], axis=1
                )
                back = dot(shaped.astype(jnp.bfloat16), w3_ref[...])
                z_real, z_imag = back[:, :lanes], back[:, lanes:]
                g_ref[at, cols] = (z_real * t_real + z_imag * t_imag).astype(jnp.bfloat16)
                g_ref[below, cols] = (z_imag * t_real - z_real * t_imag).astype(jnp.bfloat16)

        @pl.loop(0, rows_total // chunk)
        def _(step):
            at = pl.ds(pl.multiple_of(step * chunk, chunk), chunk)
            y_ref[pair, at] = dot(v1_ref[at], g_ref[...]).astype(jnp.bfloat16)

        o_ref[slot(ctx, chan, pair)] = y_ref[pair, my_rows]
        each(result_copy, pair, total, start)

    for pair in range(pairs):
        each(result_copy, pair, total, lambda copy: copy.wait_recv())

        @pl.loop(0, chan_count)
        def _(chan_index):
            first = slot(0, chan_index, pair)
            sums = []
            for i in range(ctx_count):
                for which in range(2):
                    cols = slice(which * lanes, (which + 1) * lanes)
                    carried = c_ref[first + i, :, cols].astype(jnp.float32)
                    gain = skip_ref[2 * (first + i) + which]
                    sums.append(o_ref[first + i, :, cols].astype(jnp.float32) + gain * carried)
            flat = jnp.stack(sums).reshape(group, rows * lanes)
            at = pl.ds(pl.multiple_of(first * 2, group), group)
            out_ref[at] = (gate_ref[at].astype(jnp.float32) * flat).astype(jnp.bfloat16)

    for pair in range(pairs):
        each(carried_copy, pair, total, lambda copy: copy.wait_send())
        each(spectra_copy, pair, ctx_count, lambda copy: copy.wait_send())
        each(result_copy, pair, total, lambda copy: copy.wait_send())


def channel_body(value_branch, key_branch, gate_branch, skip_gain, spectra):
    channels, tokens = value_branch.shape
    ctx_count, chan_count = lax.axis_size("ctx"), lax.axis_size("chan")
    total = ctx_count * chan_count
    rows = tokens // lanes
    rows_total = rows * total
    pairs = channels // total // 2
    local_channels = spectra.shape[1]
    block = spectra.shape[3] // lanes
    tables = [jnp.asarray(t) for t in transform_tables(rows_total, ctx_count)]
    sems = lambda *shape: pltpu.SemaphoreType.DMA(shape)
    hbm = pl.BlockSpec(memory_space=pl.ANY)
    packed = pltpu.VMEM((channels // 2, rows, 2 * lanes), jnp.bfloat16)
    held = pltpu.VMEM((channels, tokens), jnp.bfloat16)
    return pl.pallas_call(
        functools.partial(fused_kernel, ctx_count, chan_count),
        in_specs=[pl.BlockSpec(memory_space=pltpu.SMEM)] + [hbm] * 9,
        out_specs=VMEM,
        out_shape=jax.ShapeDtypeStruct((channels, tokens), jnp.bfloat16),
        scratch_shapes=[pltpu.VMEM(t.shape, t.dtype) for t in tables]
        + [
            pltpu.VMEM((2 * local_channels, block, lanes), jnp.float32),
            pltpu.VMEM((2, local_channels, block, lanes), jnp.bfloat16),
            pltpu.VMEM((2, 2 * pairs, rows_total, lanes), jnp.bfloat16),
            pltpu.VMEM((pairs, rows_total, 2 * lanes), jnp.bfloat16),
            pltpu.VMEM((pairs, rows_total, 2 * lanes), jnp.bfloat16),
            pltpu.VMEM((2 * rows_total, 2 * lanes), jnp.bfloat16),
            held, held, held, packed, packed,
        ]
        + [sems(pairs, count - 1) for count in (total, total, ctx_count, ctx_count, total, total)]
        + [sems(9)],
        compiler_params=pltpu.CompilerParams(collective_id=0, has_side_effects=True),
    )(
        skip_gain,
        value_branch,
        key_branch,
        gate_branch,
        spectra.reshape(2 * local_channels, block, lanes),
        *tables,
    )


def body(value_branch, key_branch, gate_branch, skip_gain, spectra):
    channels, tokens = value_branch.shape
    ctx_count, chan_count = lax.axis_size("ctx"), lax.axis_size("chan")
    total = ctx_count * chan_count
    block_rows = tokens * chan_count // lanes
    fits = (
        channels % (2 * total) == 0
        and ctx_count % 8 == 0
        and tokens % (16 * lanes) == 0
        and block_rows <= lanes
        and lanes % block_rows == 0
        and (tokens * total // lanes) % lanes == 0
    )
    chosen = channel_body if fits else blockwise_body
    return chosen(value_branch, key_branch, gate_branch, skip_gain, spectra)


def solution(mesh):
    in_specs = (
        P(None, ("ctx", "chan")),
        P(None, ("ctx", "chan")),
        P(None, ("ctx", "chan")),
        P(),
        P(None, "chan", "ctx", None),
    )
    out_specs = P(None, ("ctx", "chan"))
    return jax.shard_map(body, mesh=mesh, in_specs=in_specs, out_specs=out_specs, check_vma=False)
```

```python
import functools
import math

import jax
import jax.numpy as jnp
import numpy as np
from jax import lax
from jax.experimental import pallas as pl
from jax.experimental.pallas import tpu as pltpu
from jax.sharding import PartitionSpec as P

two_pi = 2.0 * math.pi
first_factor = 128
highest = lax.Precision.HIGHEST


def reversed_bits(numbers, bit_count):
    result = numbers * 0
    for bit_number in range(bit_count):
        result = result + (numbers >> bit_number & 1) * (1 << bit_count - 1 - bit_number)
    return result


def phase_pair(radians):
    return (jnp.cos(radians), jnp.sin(radians))


def block_table(length_of, direction):
    counter = jnp.arange(length_of, dtype=jnp.int32)
    product = counter[:, None] * counter[None, :] % length_of
    cosine, sine = phase_pair(direction * two_pi / length_of * product.astype(jnp.float32))
    upper_rows = jnp.stack([cosine, -sine], axis=1)
    lower_rows = jnp.stack([sine, cosine], axis=1)
    return jnp.stack([upper_rows, lower_rows], axis=0)


def complex_mul(signal, factor):
    factor_real, factor_imag = factor
    return jnp.stack(
        [
            signal[0] * factor_real - signal[1] * factor_imag,
            signal[0] * factor_imag + signal[1] * factor_real,
        ]
    )


def forward_local(signal):
    channel_count, seq_length = (signal.shape[1], signal.shape[2])
    second_factor = seq_length // first_factor
    blocked = signal.reshape(2, channel_count, first_factor, second_factor)
    section_one = jnp.einsum(
        "orca,cxaq->oxrq", block_table(first_factor, -1.0), blocked, precision=highest
    )
    column = jnp.arange(first_factor, dtype=jnp.int32)[:, None]
    within = jnp.arange(second_factor, dtype=jnp.int32)[None, :]
    twiddle = phase_pair(-two_pi / seq_length * (column * within).astype(jnp.float32))
    section_two = complex_mul(section_one, twiddle)
    section_three = jnp.einsum(
        "peoq,oxrq->pxer", block_table(second_factor, -1.0), section_two, precision=highest
    )
    return section_three.reshape(2, channel_count, seq_length)


def inverse_local(signal):
    channel_count, seq_length = (signal.shape[1], signal.shape[2])
    second_factor = seq_length // first_factor
    blocked = signal.reshape(2, channel_count, second_factor, first_factor)
    section_one = jnp.einsum(
        "pqoe,oxer->pxqr", block_table(second_factor, 1.0), blocked, precision=highest
    )
    within = jnp.arange(second_factor, dtype=jnp.int32)[:, None]
    column = jnp.arange(first_factor, dtype=jnp.int32)[None, :]
    twiddle = phase_pair(two_pi / seq_length * (within * column).astype(jnp.float32))
    section_two = complex_mul(section_one, twiddle)
    section_three = jnp.einsum(
        "paor,oxqr->pxaq", block_table(first_factor, 1.0), section_two, precision=highest
    )
    return section_three.reshape(2, channel_count, seq_length)


def blockwise_body(value_branch, key_branch, gate_branch, skip_gain, spectra):
    carried = (key_branch.astype(jnp.float32) * value_branch.astype(jnp.float32)).astype(
        jnp.bfloat16
    )
    series = lax.all_to_all(carried, "chan", split_axis=0, concat_axis=1, tiled=True)
    channel_count, seq_length = series.shape
    ctx_count = lax.axis_size("ctx")
    bit_count = ctx_count.bit_length() - 1
    device = lax.axis_index("ctx")
    total_length = seq_length * ctx_count
    counter = jnp.arange(ctx_count, dtype=jnp.int32)
    target = reversed_bits(counter, bit_count)
    blocks = lax.all_to_all(
        series.reshape(channel_count, 1, seq_length), "ctx", split_axis=2, concat_axis=1, tiled=True
    )
    matrix = jnp.stack(
        phase_pair(
            -two_pi
            / ctx_count
            * (target[:, None] * counter[None, :] % ctx_count).astype(jnp.float32)
        )
    )
    rows = jnp.einsum("ojp,xps->oxjs", matrix, blocks.astype(jnp.float32), precision=highest)
    received = lax.all_to_all(rows, "ctx", split_axis=2, concat_axis=3, tiled=True)
    signal = received.reshape(2, channel_count, seq_length)
    device_rank = reversed_bits(device, bit_count)
    positions = jnp.arange(seq_length, dtype=jnp.int32)
    radians = two_pi / total_length * (positions * device_rank).astype(jnp.float32)
    signal = complex_mul(signal, phase_pair(-radians))
    spectrum = forward_local(signal)
    shaped = complex_mul(spectrum, (spectra[0, :, 0, :], spectra[1, :, 0, :]))
    returned = complex_mul(inverse_local(shaped), phase_pair(radians))
    parts = lax.all_to_all(
        returned.reshape(2, channel_count, 1, seq_length),
        "ctx",
        split_axis=3,
        concat_axis=2,
        tiled=True,
    )
    cosine, sine = phase_pair(
        two_pi / ctx_count * (counter[:, None] * target[None, :] % ctx_count).astype(jnp.float32)
    )
    matrix = jnp.stack([cosine, -sine])
    summed = jnp.einsum("opj,oxjs->xps", matrix, parts, precision=highest) / total_length
    local_conv = summed.astype(jnp.bfloat16)
    convolved = lax.all_to_all(local_conv, "ctx", split_axis=1, concat_axis=2, tiled=True).reshape(
        channel_count, seq_length
    )
    tokens_conv = lax.all_to_all(convolved, "chan", split_axis=1, concat_axis=0, tiled=True)
    result = gate_branch.astype(jnp.float32) * (
        tokens_conv.astype(jnp.float32) + skip_gain[:, None] * carried.astype(jnp.float32)
    )
    return result.astype(jnp.bfloat16)


lanes = 128
MESH = pl.DeviceIdType.MESH
VMEM = pl.BlockSpec(memory_space=pltpu.VMEM)


@functools.lru_cache(maxsize=None)
def transform_tables(rows_total, ctx_count):
    length = rows_total * lanes
    bit_count = ctx_count.bit_length() - 1
    rev = np.array([int(format(j, "b").zfill(bit_count)[::-1], 2) if bit_count else 0 for j in range(ctx_count)])
    a = np.arange(rows_total // ctx_count)
    k1 = (rev[:, None] + ctx_count * a[None, :]).reshape(-1)
    fold = lanes // (rows_total // ctx_count)
    k2 = np.arange(lanes).reshape(lanes // fold, fold).T.reshape(-1)
    n1, n2 = np.arange(rows_total), np.arange(lanes)
    f1 = np.exp(-2j * np.pi * (np.outer(k1, n1) % rows_total) / rows_total)
    f2 = np.exp(-2j * np.pi * (np.outer(n2, k2) % lanes) / lanes)
    tw = np.exp(-2j * np.pi * (np.outer(k1, n2) % length) / length)
    w1 = np.stack([f1.real, f1.imag])
    w2 = np.block([[f2.real, f2.imag], [-f2.imag, f2.real]])
    b2 = f2.conj().T
    w3 = np.block([[b2.real, b2.imag], [-b2.imag, b2.real]])
    b1 = f1.conj().T / length
    v1 = np.concatenate([b1.real, -b1.imag], axis=1)
    half = lambda t: np.asarray(t, dtype=jnp.bfloat16)
    return half(w1), half(w2), half(w3), half(v1), np.stack([tw.real, tw.imag]).astype(np.float32)


def greet_all(ctx_count, chan_count, me):
    total = ctx_count * chan_count
    barrier = pltpu.get_barrier_semaphore()

    @pl.loop(1, total)
    def _(offset):
        other = lax.rem(me + offset, total)
        pl.semaphore_signal(
            barrier, inc=1, device_id=(other // chan_count, lax.rem(other, chan_count)), device_id_type=MESH
        )


def dot(a, b):
    return jnp.dot(a, b, preferred_element_type=jnp.float32)


def fused_kernel(ctx_count, chan_count, skip_ref, v_hbm, k_hbm, gate_hbm, s_hbm, *refs):
    tables_hbm, (out_ref,), tables = refs[:5], refs[5:6], refs[6:11]
    w1_ref, w2_ref, w3_ref, v1_ref, tw_ref = tables
    s_ref, stage, r_ref, x_ref, y_ref, g_ref = refs[11:17]
    v_ref, k_ref, gate_ref, c_ref, o_ref = refs[17:22]
    send_c, recv_c, send_s, recv_s, send_y, recv_y, local = refs[22:]
    ctx, chan = lax.axis_index("ctx"), lax.axis_index("chan")
    me = ctx * chan_count + chan
    total = ctx_count * chan_count
    pairs, rows = x_ref.shape[0], c_ref.shape[1]
    rows_total = x_ref.shape[1]
    block = stage.shape[2]
    local_channels = stage.shape[1]

    greet_all(ctx_count, chan_count, me)
    sources = (v_hbm, k_hbm, s_hbm, gate_hbm, *tables_hbm)
    targets = (v_ref, k_ref, s_ref, gate_ref, *tables)
    loads = [
        pltpu.make_async_copy(source, target, local.at[i]) for i, (source, target) in enumerate(zip(sources, targets))
    ]
    for load in loads:
        load.start()
    group = 2 * ctx_count
    loads[0].wait()
    loads[1].wait()

    def pack(pair):
        @pl.loop(0, chan_count)
        def _(chan_index):
            index = chan_index * pairs + pair
            at = pl.ds(pl.multiple_of(index * group, group), group)
            product = (k_ref[at].astype(jnp.float32) * v_ref[at].astype(jnp.float32)).astype(jnp.bfloat16)
            split = product.astype(jnp.float32).reshape(ctx_count, 2, rows, lanes)
            packed = jnp.concatenate([split[:, 0], split[:, 1]], axis=2)
            c_ref[pl.ds(index * ctx_count, ctx_count)] = packed.astype(jnp.bfloat16)


    def place(offset):
        other = lax.rem(me + offset, total)
        return other, other // chan_count, lax.rem(other, chan_count)

    def slot(ctx_index, chan_index, pair):
        return (chan_index * pairs + pair) * ctx_count + ctx_index

    my_rows = pl.ds(pl.multiple_of(me * rows, rows), rows)
    my_block = pl.ds(pl.multiple_of(ctx * block, block), block)

    def carried_copy(pair, offset):
        other, other_ctx, other_chan = place(offset)
        return pltpu.make_async_remote_copy(
            src_ref=c_ref.at[slot(other_ctx, other_chan, pair)],
            dst_ref=x_ref.at[pair, my_rows],
            send_sem=send_c.at[pair, offset - 1],
            recv_sem=recv_c.at[pair, offset - 1],
            device_id=(other_ctx, other_chan),
            device_id_type=MESH,
        )

    def spectra_copy(pair, offset):
        other_ctx = lax.rem(ctx + offset, ctx_count)
        return pltpu.make_async_remote_copy(
            src_ref=stage.at[:, pl.ds((pair * ctx_count + other_ctx) * 2, 2)],
            dst_ref=r_ref.at[:, pl.ds(2 * pair, 2), my_block],
            send_sem=send_s.at[pair, offset - 1],
            recv_sem=recv_s.at[pair, offset - 1],
            device_id=(other_ctx, chan),
            device_id_type=MESH,
        )

    def result_copy(pair, offset):
        other, other_ctx, other_chan = place(offset)
        return pltpu.make_async_remote_copy(
            src_ref=y_ref.at[pair, pl.ds(pl.multiple_of(other * rows, rows), rows)],
            dst_ref=o_ref.at[slot(ctx, chan, pair)],
            send_sem=send_y.at[pair, offset - 1],
            recv_sem=recv_y.at[pair, offset - 1],
            device_id=(other_ctx, other_chan),
            device_id_type=MESH,
        )

    def each(copy_of, pair, count, act):
        @pl.loop(1, count)
        def _(offset):
            act(copy_of(pair, offset))

    def turned(part, channel):
        flipped = s_ref[part * local_channels + channel].T
        pieces = [flipped[f * block : (f + 1) * block] for f in range(flipped.shape[0] // block)]
        return jnp.concatenate(pieces, axis=1).astype(jnp.bfloat16)

    def turn(pair):
        @pl.loop(1, ctx_count)
        def _(offset):
            first = (pair * ctx_count + lax.rem(ctx + offset, ctx_count)) * 2
            for part in range(2):
                for which in range(2):
                    stage[part, first + which] = turned(part, first + which)

        for part in range(2):
            for which in range(2):
                r_ref[part, 2 * pair + which, my_block] = turned(part, (pair * ctx_count + ctx) * 2 + which)
        x_ref[pair, my_rows] = c_ref[slot(ctx, chan, pair)]

    start = lambda copy: copy.start()
    pack(0)
    pl.semaphore_wait(pltpu.get_barrier_semaphore(), total - 1)
    each(carried_copy, 0, total, start)
    for pair in range(1, pairs):
        pack(pair)
        each(carried_copy, pair, total, start)
    loads[2].wait()
    for pair in range(pairs):
        turn(pair)
        each(spectra_copy, pair, ctx_count, start)
    for load in loads[3:]:
        load.wait()
    chunk = 2 * lanes
    for pair in range(pairs):
        each(carried_copy, pair, total, lambda copy: copy.wait_recv())
        each(spectra_copy, pair, ctx_count, lambda copy: copy.wait_recv())
        x = x_ref.at[pair]

        @pl.loop(0, rows_total // chunk)
        def _(step):
            at = pl.ds(pl.multiple_of(step * chunk, chunk), chunk)
            below = pl.ds(pl.multiple_of(rows_total + step * chunk, chunk), chunk)
            real, imag = dot(w1_ref[0, at], x[...]), dot(w1_ref[1, at], x[...])
            t_real, t_imag = tw_ref[0, at], tw_ref[1, at]
            for which in range(2):
                cols = slice(which * lanes, (which + 1) * lanes)
                a_real, a_imag = real[:, cols], imag[:, cols]
                twiddled = jnp.concatenate(
                    [a_real * t_real - a_imag * t_imag, a_real * t_imag + a_imag * t_real], axis=1
                )
                bins = dot(twiddled.astype(jnp.bfloat16), w2_ref[...])
                b_real, b_imag = bins[:, :lanes], bins[:, lanes:]
                f_real = r_ref[0, 2 * pair + which, at].astype(jnp.float32)
                f_imag = r_ref[1, 2 * pair + which, at].astype(jnp.float32)
                shaped = jnp.concatenate(
                    [b_real * f_real - b_imag * f_imag, b_real * f_imag + b_imag * f_real], axis=1
                )
                back = dot(shaped.astype(jnp.bfloat16), w3_ref[...])
                z_real, z_imag = back[:, :lanes], back[:, lanes:]
                g_ref[at, cols] = (z_real * t_real + z_imag * t_imag).astype(jnp.bfloat16)
                g_ref[below, cols] = (z_imag * t_real - z_real * t_imag).astype(jnp.bfloat16)

        @pl.loop(0, rows_total // chunk)
        def _(step):
            at = pl.ds(pl.multiple_of(step * chunk, chunk), chunk)
            y_ref[pair, at] = dot(v1_ref[at], g_ref[...]).astype(jnp.bfloat16)

        o_ref[slot(ctx, chan, pair)] = y_ref[pair, my_rows]
        each(result_copy, pair, total, start)

    for pair in range(pairs):
        each(result_copy, pair, total, lambda copy: copy.wait_recv())

        @pl.loop(0, chan_count)
        def _(chan_index):
            first = slot(0, chan_index, pair)
            sums = []
            for i in range(ctx_count):
                for which in range(2):
                    cols = slice(which * lanes, (which + 1) * lanes)
                    carried = c_ref[first + i, :, cols].astype(jnp.float32)
                    gain = skip_ref[2 * (first + i) + which]
                    sums.append(o_ref[first + i, :, cols].astype(jnp.float32) + gain * carried)
            flat = jnp.stack(sums).reshape(group, rows * lanes)
            at = pl.ds(pl.multiple_of(first * 2, group), group)
            out_ref[at] = (gate_ref[at].astype(jnp.float32) * flat).astype(jnp.bfloat16)

    for pair in range(pairs):
        each(carried_copy, pair, total, lambda copy: copy.wait_send())
        each(spectra_copy, pair, ctx_count, lambda copy: copy.wait_send())
        each(result_copy, pair, total, lambda copy: copy.wait_send())


def channel_body(value_branch, key_branch, gate_branch, skip_gain, spectra):
    channels, tokens = value_branch.shape
    ctx_count, chan_count = lax.axis_size("ctx"), lax.axis_size("chan")
    total = ctx_count * chan_count
    rows = tokens // lanes
    rows_total = rows * total
    pairs = channels // total // 2
    local_channels = spectra.shape[1]
    block = spectra.shape[3] // lanes
    tables = [jnp.asarray(t) for t in transform_tables(rows_total, ctx_count)]
    sems = lambda *shape: pltpu.SemaphoreType.DMA(shape)
    hbm = pl.BlockSpec(memory_space=pl.ANY)
    packed = pltpu.VMEM((channels // 2, rows, 2 * lanes), jnp.bfloat16)
    held = pltpu.VMEM((channels, tokens), jnp.bfloat16)
    return pl.pallas_call(
        functools.partial(fused_kernel, ctx_count, chan_count),
        in_specs=[pl.BlockSpec(memory_space=pltpu.SMEM)] + [hbm] * 9,
        out_specs=VMEM,
        out_shape=jax.ShapeDtypeStruct((channels, tokens), jnp.bfloat16),
        scratch_shapes=[pltpu.VMEM(t.shape, t.dtype) for t in tables]
        + [
            pltpu.VMEM((2 * local_channels, block, lanes), jnp.float32),
            pltpu.VMEM((2, local_channels, block, lanes), jnp.bfloat16),
            pltpu.VMEM((2, 2 * pairs, rows_total, lanes), jnp.bfloat16),
            pltpu.VMEM((pairs, rows_total, 2 * lanes), jnp.bfloat16),
            pltpu.VMEM((pairs, rows_total, 2 * lanes), jnp.bfloat16),
            pltpu.VMEM((2 * rows_total, 2 * lanes), jnp.bfloat16),
            held, held, held, packed, packed,
        ]
        + [sems(pairs, count - 1) for count in (total, total, ctx_count, ctx_count, total, total)]
        + [sems(9)],
        compiler_params=pltpu.CompilerParams(collective_id=0, has_side_effects=True),
    )(
        skip_gain,
        value_branch,
        key_branch,
        gate_branch,
        spectra.reshape(2 * local_channels, block, lanes),
        *tables,
    )


def body(value_branch, key_branch, gate_branch, skip_gain, spectra):
    channels, tokens = value_branch.shape
    ctx_count, chan_count = lax.axis_size("ctx"), lax.axis_size("chan")
    total = ctx_count * chan_count
    block_rows = tokens * chan_count // lanes
    fits = (
        channels % (2 * total) == 0
        and ctx_count % 8 == 0
        and tokens % (16 * lanes) == 0
        and block_rows <= lanes
        and lanes % block_rows == 0
        and (tokens * total // lanes) % lanes == 0
    )
    chosen = channel_body if fits else blockwise_body
    return chosen(value_branch, key_branch, gate_branch, skip_gain, spectra)


def solution(mesh):
    in_specs = (
        P(None, ("ctx", "chan")),
        P(None, ("ctx", "chan")),
        P(None, ("ctx", "chan")),
        P(),
        P(None, "chan", "ctx", None),
    )
    out_specs = P(None, ("ctx", "chan"))
    return jax.shard_map(body, mesh=mesh, in_specs=in_specs, out_specs=out_specs, check_vma=False)
```
